32 devices in a mesh: dp: 8 (over z, x), tensor: 4 (over y, core).
Axes of the slice: x: 2, y: 2, z: 4, core: 2. Of those that a mesh axis runs over, the one named last changes fastest.
Arguments:
- block_input: bfloat16 [4096, 2048], P('dp', 'tensor'), may hold values from -6 to 6
- grad_output: bfloat16 [4096, 2048], P('dp', 'tensor'), may hold values from -6 to 6
- norm_attn: float32 [2048], replicated, may hold values from 0.5 to 1.5
- norm_ffn: float32 [2048], replicated, may hold values from 0.5 to 1.5
- w_query: bfloat16 [2048, 2048], P(None, 'tensor'), may hold values from -0.125 to 0.125
- w_key: bfloat16 [2048, 2048], P(None, 'tensor'), may hold values from -0.125 to 0.125
- w_value: bfloat16 [2048, 2048], P(None, 'tensor'), may hold values from -0.125 to 0.125
- w_out: bfloat16 [2048, 2048], P('tensor'), may hold values from -0.5 to 0.5
- w_gate: bfloat16 [2048, 8192], P(None, 'tensor'), may hold values from -0.125 to 0.125
- w_up: bfloat16 [2048, 8192], P(None, 'tensor'), may hold values from -0.125 to 0.125
- w_down: bfloat16 [8192, 2048], P('tensor'), may hold values from -0.0625 to 0.0625
- doc_lengths: int32 [10], replicated, may hold values from 256 to 512, as said below
Outputs:
- block_output: bfloat16 [4096, 2048], P('dp', 'tensor')
- grad_input: bfloat16 [4096, 2048], P('dp', 'tensor')
- grad_norm_attn: float32 [2048], replicated
- grad_norm_ffn: float32 [2048], replicated
- grad_query: float32 [2048, 2048], P('dp', 'tensor')
- grad_key: float32 [2048, 2048], P('dp', 'tensor')
- grad_value: float32 [2048, 2048], P('dp', 'tensor')
- grad_out_proj: float32 [2048, 2048], P('tensor', 'dp')
- grad_gate: float32 [2048, 8192], P('dp', 'tensor')
- grad_up: float32 [2048, 8192], P('dp', 'tensor')
- grad_down: float32 [8192, 2048], P('tensor', 'dp')
The draws below stay inside these ranges and needn't reach their ends.
Inputs may be any that keep to these rules, and one draw needn't show every extreme that they name: `doc_lengths`: every 2048 tokens in order form a row of exactly 5 whole documents; the first of each row has 512 tokens.
All inputs are finite; a program needn't handle non-finite values.
Results may differ from the reference program's by a relative error of at most 0.014.
Values may be sent and summed in bfloat16 or wider, within the bound.
A program may use at most 320 MiB of HBM per device.

```python
import jax
import jax.numpy as jnp
from jax import lax

D = 2048
HEADS = 32
HEAD_DIM = 64
FF = 8192
ROW_LEN = 2048
BLK = 128
TOKENS = 4096
RECV = 1024
N_DP = 8


def draw_doc_lengths(key, part):
    row_count = TOKENS // ROW_LEN
    spread = ROW_LEN // 16
    middle = 3 * ROW_LEN // 16
    plan_key = jax.random.fold_in(key, 31)
    key_spread = jax.random.fold_in(plan_key, 1)
    key_order = jax.random.fold_in(plan_key, 2)
    shifts = jax.random.randint(key_spread, (row_count, 2), -spread, spread + 1, dtype=jnp.int32)
    longest = jnp.full((row_count, 1), ROW_LEN // 4, jnp.int32)
    others = jnp.stack([middle + shifts[:, 0], middle - shifts[:, 0], middle + shifts[:, 1], middle - shifts[:, 1]], axis=1)
    ranking = jax.random.randint(key_order, (row_count, 4), 0, 1 << 20, dtype=jnp.int32) * 8 + jnp.arange(4, dtype=jnp.int32)[None, :]
    row_order = jnp.argsort(ranking, axis=1)
    shuffled = jnp.take_along_axis(others, row_order, axis=1)
    return jnp.concatenate([longest, shuffled], axis=1).reshape(-1).astype(jnp.int32)


def block_levels(rng, shape, cuts, least, largest):
    level = 1.0
    for dim, blocks in cuts:
        draws = jax.random.uniform(jax.random.fold_in(jax.random.fold_in(rng, 6), dim), (blocks,), jnp.float32, least / len(cuts), largest / len(cuts))
        level = level * jnp.repeat(jnp.exp(draws), shape[dim] // blocks).reshape((-1,) + (1,) * (len(shape) - 1 - dim))
    return level


def scatter_about(stream_key, dims, scale, reach, shards=(), held_as=jnp.bfloat16):
    values = jax.random.normal(stream_key, dims, jnp.float32) * scale
    if len(shards) > 0:
        values = block_levels(stream_key, dims, shards, -0.22, 0.18) * values
    return jnp.clip(values, min=-reach, max=reach).astype(held_as)


def setup_inputs(seed: int = 0) -> dict:
    key_list = jax.random.split(jax.random.key(seed), 13)
    return {
        "block_input": scatter_about(key_list[0], (TOKENS, D), 1.0, 6.0, ((0, 8), (1, 4))),
        "grad_output": scatter_about(key_list[1], (TOKENS, D), 1.0, 6.0, ((0, 8), (1, 4))),
        "norm_attn": jnp.clip(1.0 + 0.1 * jax.random.normal(key_list[2], (D,), jnp.float32), 0.5, 1.5),
        "norm_ffn": jnp.clip(1.0 + 0.1 * jax.random.normal(key_list[3], (D,), jnp.float32), 0.5, 1.5),
        "w_query": scatter_about(key_list[4], (D, HEADS * HEAD_DIM), D ** -0.5, 0.125, ((1, 4),)),
        "w_key": scatter_about(key_list[5], (D, HEADS * HEAD_DIM), D ** -0.5, 0.125, ((1, 4),)),
        "w_value": scatter_about(key_list[6], (D, HEADS * HEAD_DIM), D ** -0.5, 0.125, ((1, 4),)),
        "w_out": scatter_about(key_list[7], (HEADS * HEAD_DIM, D), (HEADS * HEAD_DIM // 16) ** -0.5, 0.5, ((0, 4),)),
        "w_gate": scatter_about(key_list[8], (D, FF), D ** -0.5, 0.125, ((1, 4),)),
        "w_up": scatter_about(key_list[9], (D, FF), D ** -0.5, 0.125, ((1, 4),)),
        "w_down": scatter_about(key_list[10], (FF, D), FF ** -0.5, 0.0625, ((0, 4),)),
        "doc_lengths": draw_doc_lengths(jax.random.fold_in(key_list[12], 71), 0),
    }


EPS = 1e-05
THETA = 130000.0
MASKED = -1000000000.0

@jax.custom_vjp
def low(v):
    return lax.optimization_barrier(v.astype(jnp.bfloat16)).astype(jnp.float32)

@jax.custom_vjp
def low_back(v):
    return v

def low_keep(v):
    return (low(v), None)

def low_pass(kept, grad):
    return (grad,)

def back_keep(v):
    return (v, None)

def back_low(kept, grad):
    return (low(grad),)
low.defvjp(low_keep, low_pass)
low_back.defvjp(back_keep, back_low)

def product(left, right):
    return jnp.dot(left, right, precision=lax.Precision.HIGHEST)

def assign_groups(doc_lengths, group_count):
    doc_count = doc_lengths.shape[0]
    doc_ids = jnp.arange(doc_count, dtype=jnp.int32)
    priority = (ROW_LEN - doc_lengths).astype(jnp.int32) * doc_count + doc_ids
    doc_rank = lax.optimization_barrier(jnp.sum((priority[None, :] < priority[:, None]).astype(jnp.int32), axis=1, dtype=jnp.int32))
    rounds = doc_rank // group_count
    within = doc_rank % group_count
    dealt = jnp.where(rounds % 2 == 0, within, group_count - 1 - within)
    return ((dealt + 1) % group_count).astype(jnp.int32)

def doc_tables(doc_lengths, doc_groups, group_id, capacity, block_pad):
    starts = jnp.cumsum(doc_lengths, dtype=jnp.int32) - doc_lengths
    padded = (doc_lengths + block_pad - 1) // block_pad * block_pad
    owned = doc_groups == group_id
    owned_pad = jnp.where(owned, padded, 0).astype(jnp.int32)
    rstart = jnp.cumsum(owned_pad, dtype=jnp.int32) - owned_pad
    buffer_pos = jnp.arange(capacity, dtype=jnp.int32)[:, None]
    inside = owned[None, :] & (buffer_pos >= rstart[None, :]) & (buffer_pos < rstart[None, :] + doc_lengths[None, :])
    offsets = buffer_pos - rstart[None, :]
    filled = jnp.any(inside, axis=1)
    source = lax.optimization_barrier(jnp.sum(jnp.where(inside, starts[None, :] + offsets, 0), axis=1, dtype=jnp.int32))
    position = lax.optimization_barrier(jnp.sum(jnp.where(inside, offsets, 0), axis=1, dtype=jnp.int32))
    doc_ids = jnp.arange(doc_lengths.shape[0], dtype=jnp.int32)
    owner_doc = lax.optimization_barrier(jnp.sum(jnp.where(inside, doc_ids[None, :], 0), axis=1, dtype=jnp.int32))
    segment = jnp.where(filled, owner_doc, -1 - buffer_pos[:, 0])
    return (filled, source, position, segment)

def rope_tables(position, head_dim):
    half_dim = head_dim // 2
    frequency = THETA ** (-jnp.arange(half_dim, dtype=jnp.float32) * 2.0 / head_dim)
    angles = position.astype(jnp.float32)[:, None] * frequency[None, :]
    return (jnp.cos(angles)[:, None, :], jnp.sin(angles)[:, None, :])

def rotate(values, cosine, sine, turn):
    half_dim = values.shape[-1] // 2
    front_half = values[..., :half_dim]
    back_half = values[..., half_dim:]
    return jnp.concatenate([front_half * cosine - turn * back_half * sine, back_half * cosine + turn * front_half * sine], axis=-1)

def layer(block, weights, position, segment):
    norm_one, norm_two, w_query, w_key, w_value, w_out, w_gate, w_up, w_down = weights
    capacity = block.shape[0]
    scale_one = lax.rsqrt(lax.optimization_barrier(jnp.mean(block * block, axis=1, keepdims=True)) + EPS)
    normed_one = low(block * scale_one * norm_one)
    cosine, sine = rope_tables(position, HEAD_DIM)
    query = low_back(product(normed_one, w_query)).reshape(capacity, -1, HEAD_DIM)
    query = low(rotate(query, cosine, sine, 1.0))
    keys = low_back(product(normed_one, w_key)).reshape(capacity, -1, HEAD_DIM)
    keys = low(rotate(keys, cosine, sine, 1.0))
    values = low(low_back(product(normed_one, w_value))).reshape(capacity, -1, HEAD_DIM)
    scores = jnp.einsum('qhd,khd->hqk', query, keys, precision=lax.Precision.HIGHEST) * HEAD_DIM ** (-0.5)
    scores = low_back(scores)
    row_at = jnp.arange(capacity, dtype=jnp.int32)[:, None]
    col_at = jnp.arange(capacity, dtype=jnp.int32)[None, :]
    allowed = (segment[:, None] == segment[None, :]) & (col_at <= row_at)
    scores = jnp.where(allowed[None], scores, MASKED)
    row_peak = lax.optimization_barrier(jnp.max(scores, axis=-1, keepdims=True))
    exponent = jnp.exp(scores - row_peak)
    prob = low(exponent / lax.optimization_barrier(jnp.sum(exponent, axis=-1, keepdims=True)))
    attended = jnp.einsum('hqk,khd->qhd', prob, values, precision=lax.Precision.HIGHEST).reshape(capacity, -1)
    attended = low(low_back(attended))
    hidden_state = block + low_back(product(attended, w_out))
    scale_two = lax.rsqrt(lax.optimization_barrier(jnp.mean(hidden_state * hidden_state, axis=1, keepdims=True)) + EPS)
    normed_two = low(hidden_state * scale_two * norm_two)
    gate_proj = low_back(product(normed_two, w_gate))
    up_proj = low_back(product(normed_two, w_up))
    inner = low(jax.nn.silu(gate_proj) * up_proj)
    return hidden_state + low_back(product(inner, w_down))

def reference(block_input, grad_output, norm_attn, norm_ffn, w_query, w_key, w_value, w_out, w_gate, w_up, w_down, doc_lengths):
    token_count = block_input.shape[0]
    model_width = block_input.shape[1]
    doc_groups = assign_groups(doc_lengths, N_DP)
    inputs_f = block_input.astype(jnp.float32)
    grads_f = grad_output.astype(jnp.float32)
    params = (norm_attn.astype(jnp.float32), norm_ffn.astype(jnp.float32), w_query.astype(jnp.float32), w_key.astype(jnp.float32), w_value.astype(jnp.float32), w_out.astype(jnp.float32), w_gate.astype(jnp.float32), w_up.astype(jnp.float32), w_down.astype(jnp.float32))

    def per_group(carry, group_id):
        outputs_all, inputs_grad_all, sums = carry
        filled, source, position, segment = doc_tables(doc_lengths, doc_groups, group_id, RECV, BLK)
        keep_rows = filled[:, None]
        block = jnp.where(keep_rows, inputs_f[source], jnp.float32(0.0))
        cotangent = jnp.where(keep_rows, grads_f[source], jnp.float32(0.0))

        def run(block_in, weights):
            return layer(block_in, weights, position, segment)
        result, pull = jax.vjp(run, block, params)
        grad_block, grad_params = pull(cotangent)
        target = jnp.where(filled, source, token_count).astype(jnp.int32)
        outputs_all = outputs_all.at[target].set(result)
        inputs_grad_all = inputs_grad_all.at[target].set(grad_block)
        sums = jax.tree.map(lambda summed, fresh: summed + fresh, sums, grad_params)
        return ((outputs_all, inputs_grad_all, sums), None)
    start_sums = jax.tree.map(lambda array: jnp.zeros(array.shape, jnp.float32), params)
    start = (jnp.zeros((token_count + 1, model_width), jnp.float32), jnp.zeros((token_count + 1, model_width), jnp.float32), start_sums)
    final, unused = lax.scan(per_group, start, jnp.arange(N_DP, dtype=jnp.int32))
    outputs_all, inputs_grad_all, sums = final
    return (outputs_all[:token_count].astype(jnp.bfloat16), inputs_grad_all[:token_count].astype(jnp.bfloat16), sums[0], sums[1], sums[2], sums[3], sums[4], sums[5], sums[6], sums[7], sums[8])
```

```python
import jax
import jax.numpy as jnp
from jax import lax
from jax.sharding import PartitionSpec as P

HEAD_DIM = 64
ROW_LEN = 2048
EPS = 1e-05
THETA = 130000.0
MASKED = -1000000000.0
RING = 4

F32 = jnp.float32
LOW = jnp.bfloat16


def mm(left, right, lc, rc):
    return lax.dot_general(left, right, (((lc,), (rc,)), ((), ())), preferred_element_type=F32)


def bits_of(size):
    step = size // 2
    while step:
        yield step
        step //= 2


def swap(values, axis, mask):
    count = lax.axis_size(axis)
    return lax.ppermute(values, axis, [(i, i ^ mask) for i in range(count)])


def sum_all(values, axis, masks):
    for mask in masks:
        values = values + swap(values, axis, mask)
    return values


def gather_features(part):
    count = lax.axis_size("tensor")
    me = lax.axis_index("tensor")
    rows, width = part.shape
    held = {0: part}
    for mask in bits_of(count):
        held.update({mask | at: swap(block, "tensor", mask) for at, block in list(held.items())})
    whole = jnp.zeros((rows, count * width), part.dtype)
    for at, block in held.items():
        whole = lax.dynamic_update_slice(whole, block, (0, (me ^ at) * width))
    return whole


def scatter_features(product):
    count = lax.axis_size("tensor")
    me = lax.axis_index("tensor")
    core = me % 2
    chip = me // 2
    sent = product(1 - core).astype(LOW)
    got = swap(sent, "tensor", 1)
    kept = product(core) + got.astype(F32)
    chips = count // 2
    width = kept.shape[1] // chips
    total = None
    for mask in range(1, chips):
        other = lax.dynamic_slice_in_dim(kept, (chip ^ mask) * width, width, 1).astype(LOW)
        come = swap(other, "tensor", mask * 2).astype(F32)
        total = come if total is None else total + come
    mine = lax.dynamic_slice_in_dim(kept, chip * width, width, 1)
    return mine if total is None else mine + total


def core_columns(weight, core):
    count = lax.axis_size("tensor")
    rows, cols = weight.shape
    view = weight.reshape(rows, count // 2, 2, cols // count)
    return lax.dynamic_index_in_dim(view, core, 2, False).reshape(rows, cols // 2)


def core_rows(weight, core):
    count = lax.axis_size("tensor")
    rows, cols = weight.shape
    view = weight.reshape(count // 2, 2, rows // count, cols)
    return lax.dynamic_index_in_dim(view, core, 1, False).reshape(rows // 2, cols)


def rope_tables(position):
    half_dim = HEAD_DIM // 2
    frequency = THETA ** (-jnp.arange(half_dim, dtype=F32) * 2.0 / HEAD_DIM)
    angles = position.astype(F32)[:, None] * frequency[None, :]
    return (jnp.cos(angles)[:, None, :], jnp.sin(angles)[:, None, :])


def rotate(values, cosine, sine, turn):
    half_dim = values.shape[-1] // 2
    front_half = values[..., :half_dim]
    back_half = values[..., half_dim:]
    return jnp.concatenate(
        [
            front_half * cosine - turn * back_half * sine,
            back_half * cosine + turn * front_half * sine,
        ],
        axis=-1,
    )


def per_device(
    block_input,
    grad_output,
    norm_attn,
    norm_ffn,
    w_query,
    w_key,
    w_value,
    w_out,
    w_gate,
    w_up,
    w_down,
    doc_lengths,
):
    tok, width = block_input.shape
    width_all = norm_attn.shape[0]
    n_dp = lax.axis_size("dp")
    me = lax.axis_index("dp")
    shard = lax.axis_index("tensor")
    ring = min(RING, n_dp // 2)
    blocks = n_dp // (2 * ring)
    pair_at = me % 2
    ring_at = (me // 2) % ring
    block_at = me // (2 * ring)
    owned = width_all // n_dp

    def ring_step(values):
        pairs = []
        for i in range(n_dp):
            b, k, c = i // (2 * ring), (i // 2) % ring, i % 2
            pairs.append((i, (b * ring + (k + 1) % ring) * 2 + c))
        return lax.ppermute(values, "dp", pairs)

    row_groups = ROW_LEN // tok
    halo_pairs = [
        (i, i + 1) for i in range(n_dp) if 0 < i % row_groups < row_groups - 1
    ]
    back_pairs = [(j, i) for i, j in halo_pairs]

    starts = jnp.cumsum(doc_lengths, dtype=jnp.int32) - doc_lengths
    token_ids = me * tok + jnp.arange(tok, dtype=jnp.int32)
    doc_start = jnp.max(
        jnp.where(starts[None, :] <= token_ids[:, None], starts[None, :], 0), axis=1
    )
    position = token_ids - doc_start
    cosine, sine = rope_tables(position)

    my_gain_one = lax.dynamic_slice_in_dim(norm_attn, shard * width, width)
    my_gain_two = lax.dynamic_slice_in_dim(norm_ffn, shard * width, width)

    rows_low = gather_features(block_input)
    rows_in = rows_low.astype(F32)
    scale_one = lax.rsqrt(jnp.mean(rows_in * rows_in, axis=1, keepdims=True) + EPS)
    normed_one = (rows_in * scale_one * norm_attn).astype(LOW)
    my_rows = block_input.astype(F32)
    my_grad = grad_output.astype(F32)

    grad_low = gather_features(grad_output)

    heads = w_query.shape[1] // HEAD_DIM
    key_f = mm(normed_one, w_key, 1, 0).reshape(tok, heads, HEAD_DIM)
    key_low = rotate(key_f, cosine, sine, 1.0).astype(LOW)
    value_low = mm(normed_one, w_value, 1, 0).astype(LOW).reshape(tok, heads, HEAD_DIM)
    halo_key = lax.ppermute(key_low, "dp", halo_pairs)
    halo_value = lax.ppermute(value_low, "dp", halo_pairs)
    query_f = mm(normed_one, w_query, 1, 0).reshape(tok, heads, HEAD_DIM)
    query_low = rotate(query_f, cosine, sine, 1.0).astype(LOW)

    score_scale = HEAD_DIM ** (-0.5)
    keys = jnp.concatenate([halo_key, key_low], axis=0)
    values = jnp.concatenate([halo_value, value_low], axis=0)
    key_ids = (me - 1) * tok + jnp.arange(2 * tok, dtype=jnp.int32)
    allowed = (key_ids[None, :] >= doc_start[:, None]) & (key_ids[None, :] <= token_ids[:, None])
    scores = jnp.einsum("qhd,khd->hqk", query_low, keys, preferred_element_type=F32) * score_scale
    scores = jnp.where(allowed[None], scores, MASKED)
    peak = jnp.max(scores, axis=-1, keepdims=True)
    exponent = jnp.exp(scores - peak)
    mass = jnp.sum(exponent, axis=-1, keepdims=True)
    prob_low = (exponent / mass).astype(LOW)
    log_sum = peak + jnp.log(mass)
    attended = (
        jnp.einsum("hqk,khd->qhd", prob_low, values, preferred_element_type=F32)
        .reshape(tok, heads * HEAD_DIM)
        .astype(LOW)
    )

    hidden = my_rows + scatter_features(lambda core: mm(attended, core_columns(w_out, core), 1, 0))
    tensor_masks = [1 << i for i in range((lax.axis_size("tensor") - 1).bit_length())]
    square = sum_all(jnp.sum(hidden * hidden, axis=1), "tensor", tensor_masks)
    scale_two = lax.rsqrt(square / width_all + EPS)[:, None]
    normed_slice = (hidden * scale_two * my_gain_two).astype(LOW)
    normed_two = gather_features(normed_slice)

    gate = mm(normed_two, w_gate, 1, 0)
    up = mm(normed_two, w_up, 1, 0)
    sig = jax.nn.sigmoid(gate)
    inner = (gate * sig * up).astype(LOW)
    ffn = scatter_features(lambda core: mm(inner, core_columns(w_down, core), 1, 0))
    block_output = (hidden + ffn).astype(LOW)

    def ffn_back(gate, up, sig, grads):
        d_inner = mm(grads, w_down, 1, 1)
        d_gate = (d_inner * up * sig * (1.0 + gate * (1.0 - sig))).astype(LOW)
        d_up = (d_inner * gate * sig).astype(LOW)
        return d_gate, d_up

    d_gate, d_up = ffn_back(gate, up, sig, grad_low)
    d_normed_two = scatter_features(
        lambda core: mm(d_gate, core_rows(w_gate, core), 1, 1)
        + mm(d_up, core_rows(w_up, core), 1, 1)
    )
    gain_two = jnp.sum(d_normed_two * hidden * scale_two, axis=0)
    weighted = d_normed_two * my_gain_two
    mean_two = sum_all(jnp.sum(weighted * hidden, axis=1), "tensor", tensor_masks) / width_all
    d_hidden = my_grad + scale_two * (
        weighted - hidden * scale_two * scale_two * mean_two[:, None]
    )
    d_hidden_low = gather_features(d_hidden.astype(LOW))

    normed_parts, grad_parts = [], []
    normed_at, grad_at = normed_slice, grad_output
    for _ in range(ring - 1):
        grad_at = ring_step(grad_at)
        grad_parts.append(gather_features(grad_at))
    for _ in range(ring - 1):
        normed_at = ring_step(normed_at)
        normed_parts.append(gather_features(normed_at))
    far_normed = jnp.concatenate(normed_parts, axis=0)
    far_grad = jnp.concatenate(grad_parts, axis=0)
    far_gate = mm(far_normed, w_gate, 1, 0)
    far_up = mm(far_normed, w_up, 1, 0)
    far_sig = jax.nn.sigmoid(far_gate)
    far_inner = (far_gate * far_sig * far_up).astype(LOW)
    far_d_gate, far_d_up = ffn_back(far_gate, far_up, far_sig, far_grad)

    def owned_columns(rows, at):
        view = rows.reshape(rows.shape[0], blocks, ring, 2, owned)
        view = lax.dynamic_index_in_dim(view, at // 2, 1, False)
        view = lax.dynamic_index_in_dim(view, ring_at, 1, False)
        return lax.dynamic_index_in_dim(view, at % 2, 1, False)

    seat = block_at * 2 + pair_at
    seats = blocks * 2

    def seat_swap(values, mask):
        pairs = []
        for i in range(n_dp):
            b, k, c = i // (2 * ring), (i // 2) % ring, i % 2
            s = (b * 2 + c) ^ mask
            pairs.append((i, ((s // 2) * ring + k) * 2 + s % 2))
        return lax.ppermute(values, "dp", pairs)

    def ffn_weight_grad(near_rows, far_rows, near_units, far_units, units_first):
        def part(at):
            near = owned_columns(near_rows, at)
            far = owned_columns(far_rows, at)
            if units_first:
                return mm(far_units, far, 0, 0) + mm(near_units, near, 0, 0)
            return mm(far, far_units, 0, 0) + mm(near, near_units, 0, 0)

        come = [
            seat_swap(part(seat ^ mask).astype(LOW), mask) for mask in range(1, seats)
        ]
        total = part(seat)
        for value in come:
            total = total + value.astype(F32)
        return total

    grad_down = ffn_weight_grad(grad_low, far_grad, inner, far_inner, True)
    grad_gate = ffn_weight_grad(normed_two, far_normed, d_gate, far_d_gate, False)
    grad_up = ffn_weight_grad(normed_two, far_normed, d_up, far_d_up, False)

    d_attended = mm(d_hidden_low, w_out, 1, 1).astype(LOW).reshape(tok, heads, HEAD_DIM)
    scores = jnp.einsum("qhd,khd->hqk", query_low, keys, preferred_element_type=F32) * score_scale
    scores = jnp.where(allowed[None], scores, MASKED)
    prob = jnp.exp(scores - log_sum)
    d_values = jnp.einsum("hqk,qhd->khd", prob.astype(LOW), d_attended, preferred_element_type=F32)
    d_prob = jnp.einsum("qhd,khd->hqk", d_attended, values, preferred_element_type=F32)
    delta = jnp.sum(prob * d_prob, axis=-1, keepdims=True)
    d_scores = (prob * (d_prob - delta)).astype(LOW)
    d_query_rot = (
        jnp.einsum("hqk,khd->qhd", d_scores, keys, preferred_element_type=F32) * score_scale
    )
    d_keys_rot = (
        jnp.einsum("hqk,qhd->khd", d_scores, query_low, preferred_element_type=F32) * score_scale
    )
    back_key = lax.ppermute(d_keys_rot[:tok].astype(LOW), "dp", back_pairs)
    back_value = lax.ppermute(d_values[:tok].astype(LOW), "dp", back_pairs)
    d_key_rot = d_keys_rot[tok:] + back_key.astype(F32)
    d_value_f = d_values[tok:] + back_value.astype(F32)
    flat = (tok, heads * HEAD_DIM)
    d_query = rotate(d_query_rot, cosine, sine, -1.0).astype(LOW).reshape(flat)
    d_key = rotate(d_key_rot, cosine, sine, -1.0).astype(LOW).reshape(flat)
    d_value = d_value_f.astype(LOW).reshape(flat)

    d_normed_one = scatter_features(
        lambda core: mm(d_query, core_rows(w_query, core), 1, 1)
        + mm(d_key, core_rows(w_key, core), 1, 1)
        + mm(d_value, core_rows(w_value, core), 1, 1)
    )
    gain_one = jnp.sum(d_normed_one * my_rows * scale_one, axis=0)
    weighted = d_normed_one * my_gain_one
    mean_one = sum_all(jnp.sum(weighted * my_rows, axis=1), "tensor", tensor_masks) / width_all
    d_rows = d_hidden + scale_one * (
        weighted - my_rows * scale_one * scale_one * mean_one[:, None]
    )
    grad_input = d_rows.astype(LOW)

    def attn_weight_grad(rows, units, units_first):
        pieces = rows.reshape(tok, blocks, ring, 2, owned)

        def part(at):
            mine = lax.dynamic_index_in_dim(pieces, at, 3, False).reshape(tok, -1)
            return mm(units, mine, 0, 0) if units_first else mm(mine, units, 0, 0)

        def split(values):
            if units_first:
                return values.reshape(-1, blocks, ring, owned)
            return values.reshape(blocks, ring, owned, -1)

        axis = 2 if units_first else 1
        come = swap(part(1 - pair_at).astype(LOW), "dp", 1)
        total = split(part(pair_at) + come.astype(F32))
        moving = None
        for step in range(1, ring + 1):
            at = (ring_at - step) % ring
            term = lax.dynamic_index_in_dim(total, at, axis, False)
            moving = term if moving is None else moving.astype(F32) + term
            if step < ring:
                moving = ring_step(moving.astype(LOW))
        axis = 1 if units_first else 0
        mine = lax.dynamic_index_in_dim(moving, block_at, axis, False)
        for mask in range(1, blocks):
            other = lax.dynamic_index_in_dim(moving, block_at ^ mask, axis, False)
            come = swap(other.astype(LOW), "dp", mask * 2 * ring)
            mine = mine + come.astype(F32)
        return mine

    grad_wout = attn_weight_grad(d_hidden_low, attended, True)
    grad_query = attn_weight_grad(normed_one, d_query, False)
    grad_key = attn_weight_grad(normed_one, d_key, False)
    grad_value = attn_weight_grad(normed_one, d_value, False)

    gains = jnp.stack([gain_one, gain_two])
    gains = sum_all(gains, "dp", [1 << i for i in range((n_dp - 1).bit_length())])
    gains = gather_features(gains)
    return (
        block_output,
        grad_input,
        gains[0],
        gains[1],
        grad_query,
        grad_key,
        grad_value,
        grad_wout,
        grad_gate,
        grad_up,
        grad_down,
    )


def solution(mesh):
    return jax.shard_map(
        per_device,
        mesh=mesh,
        in_specs=(
            P("dp", "tensor"),
            P("dp", "tensor"),
            P(),
            P(),
            P(None, "tensor"),
            P(None, "tensor"),
            P(None, "tensor"),
            P("tensor", None),
            P(None, "tensor"),
            P(None, "tensor"),
            P("tensor", None),
            P(),
        ),
        out_specs=(
            P("dp", "tensor"),
            P("dp", "tensor"),
            P(),
            P(),
            P("dp", "tensor"),
            P("dp", "tensor"),
            P("dp", "tensor"),
            P("tensor", "dp"),
            P("dp", "tensor"),
            P("dp", "tensor"),
            P("tensor", "dp"),
        ),
        check_vma=False,
    )
```

```python
import functools

import jax
import jax.numpy as jnp
from jax import lax
from jax.experimental import pallas as pl
from jax.experimental.pallas import tpu as pltpu
from jax.sharding import Mesh
from jax.sharding import PartitionSpec as P

HEAD_DIM = 64
PAIR = 2 * HEAD_DIM
ROW_LEN = 2048
MAX_DOC = 512
EPS = 1e-05
THETA = 130000.0
MASKED = -1000000000.0
RING = 4
SCORE_SCALE = HEAD_DIM ** (-0.5)

DP = ("block", "ring", "pair")
TP = ("chip", "core")

F32 = jnp.float32
LOW = jnp.bfloat16


def mm(left, right, lc, rc):
    return lax.dot_general(left, right, (((lc,), (rc,)), ((), ())), preferred_element_type=F32)


def shape_of(dims, kind):
    return jax.ShapeDtypeStruct(dims, kind)


def cost(flops, moved, transcendentals=0):
    return pl.CostEstimate(flops=flops, bytes_accessed=moved, transcendentals=transcendentals)


def whole_spec(dims):
    return pl.BlockSpec(dims, lambda *_: (0,) * len(dims), pipeline_mode=pl.Buffered(1))


def bits_of(size):
    step = size // 2
    while step:
        yield step
        step //= 2


def swap(values, axis, mask):
    count = lax.axis_size(axis)
    return lax.ppermute(values, axis, [(i, i ^ mask) for i in range(count)])


def sum_all(values, axis):
    for at in range((lax.axis_size(axis) - 1).bit_length()):
        values = values + swap(values, axis, 1 << at)
    return values


def gather_blocks(part):
    held = {0: part}
    for mask in bits_of(lax.axis_size(TP)):
        held.update({mask | at: swap(block, TP, mask) for at, block in list(held.items())})
    return [held[at] for at in range(len(held))]


def turn(values, cosine, sine, sign):
    lanes = values.shape[1]
    reps = lanes // PAIR
    if reps > 1:
        cosine = jnp.tile(cosine, (1, reps))
        sine = jnp.tile(sine, (1, reps))
    half = HEAD_DIM // 2
    lane = lax.broadcasted_iota(jnp.int32, values.shape, 1)
    ahead = pltpu.roll(values, lanes - half, 1)
    behind = pltpu.roll(values, half, 1)
    other = jnp.where(lane % HEAD_DIM < half, -ahead, behind)
    return values * cosine + (sign * other) * sine


def split_pairs(rows, owned, odd, keep, send):
    for at in range(rows.shape[1] // (2 * owned)):
        first = rows[:, 2 * at * owned : (2 * at + 1) * owned]
        second = rows[:, (2 * at + 1) * owned : (2 * at + 2) * owned]
        keep[:, at * owned : (at + 1) * owned] = jnp.where(odd, second, first)
        send[:, at * owned : (at + 1) * owned] = jnp.where(odd, first, second)


def norm_rows(blocks, normed, gain, shard):
    width = blocks[0].shape[1]
    total = None
    for block in blocks:
        value = block[...].astype(F32)
        part = jnp.sum(value * value, axis=1, keepdims=True)
        total = part if total is None else total + part
    scale = lax.rsqrt(total / (len(blocks) * width) + EPS)
    for at, block in enumerate(blocks):
        cols = pl.ds(pl.multiple_of((shard ^ at) * width, width), width)
        normed[:, cols] = (block[...].astype(F32) * scale * gain[:, cols]).astype(LOW)
    return scale


def project_in_kernel(count, owned, index, *refs):
    blocks = refs[:count]
    gain, cosine, sine, w_query, w_key, w_value = refs[count : count + 6]
    query, both, keep, send, scale_out, normed = refs[count + 6 :]
    scale = norm_rows(blocks, normed, gain, index[0])
    scale_out[...] = jnp.broadcast_to(scale, scale_out.shape)
    split_pairs(normed, owned, index[1] == 1, keep, send)
    rows = normed[...]
    key = mm(rows, w_key[...], 1, 0)
    both[0] = turn(key, cosine[...], sine[...], 1.0).astype(LOW)
    both[1] = mm(rows, w_value[...], 1, 0).astype(LOW)
    asked = turn(mm(rows, w_query[...], 1, 0), cosine[...], sine[...], 1.0).astype(LOW)
    query[...] = (asked.astype(F32) * SCORE_SCALE).astype(LOW)


def project_in(blocks, gain, cosine, sine, w_query, w_key, w_value, index, owned):
    count = len(blocks)
    tok, width = blocks[0].shape
    wide, local = w_query.shape
    step = min(256, tok)
    row = lambda cols: pl.BlockSpec((step, cols), lambda i, s: (i, 0))
    return pl.pallas_call(
        functools.partial(project_in_kernel, count, owned),
        grid_spec=pltpu.PrefetchScalarGridSpec(
            num_scalar_prefetch=1,
            grid=(tok // step,),
            in_specs=[row(width)] * count
            + [whole_spec((1, wide)), row(PAIR), row(PAIR)]
            + [whole_spec((wide, local))] * 3,
            out_specs=[
                row(local),
                pl.BlockSpec((2, step, local), lambda i, s: (0, i, 0)),
                row(wide // 2),
                row(wide // 2),
                row(128),
            ],
            scratch_shapes=[pltpu.VMEM((step, wide), LOW)],
        ),
        out_shape=[
            shape_of((tok, local), LOW),
            shape_of((2, tok, local), LOW),
            shape_of((tok, wide // 2), LOW),
            shape_of((tok, wide // 2), LOW),
            shape_of((tok, 128), F32),
        ],
        cost_estimate=cost(6 * tok * wide * local, 6 * wide * local + 12 * tok * wide),
        name="project_in",
    )(index, *blocks, gain[None, :], cosine, sine, w_query, w_key, w_value)


def project_halo_kernel(count, index, *refs):
    blocks = refs[:count]
    gain, cosine, sine, w_key, w_value, both, normed = refs[count:]
    norm_rows(blocks, normed, gain, index[0])
    rows = normed[...]
    key = mm(rows, w_key[...], 1, 0)
    both[0] = turn(key, cosine[...], sine[...], 1.0).astype(LOW)
    both[1] = mm(rows, w_value[...], 1, 0).astype(LOW)


def project_halo(blocks, gain, cosine, sine, w_key, w_value, index):
    count = len(blocks)
    tok, width = blocks[0].shape
    wide, local = w_key.shape
    step = min(256, tok)
    row = lambda cols: pl.BlockSpec((step, cols), lambda i, s: (i, 0))
    return pl.pallas_call(
        functools.partial(project_halo_kernel, count),
        grid_spec=pltpu.PrefetchScalarGridSpec(
            num_scalar_prefetch=1,
            grid=(tok // step,),
            in_specs=[row(width)] * count
            + [whole_spec((1, wide)), row(PAIR), row(PAIR)]
            + [whole_spec((wide, local))] * 2,
            out_specs=pl.BlockSpec((2, step, local), lambda i, s: (0, i, 0)),
            scratch_shapes=[pltpu.VMEM((step, wide), LOW)],
        ),
        out_shape=shape_of((2, tok, local), LOW),
        cost_estimate=cost(4 * tok * wide * local, 4 * wide * local + 6 * tok * wide),
        name="project_halo",
    )(index, *blocks, gain[None, :], cosine, sine, w_key, w_value)


def two_heads(values):
    lane = lax.broadcasted_iota(jnp.int32, values.shape, 1)
    zero = jnp.zeros_like(values)
    first = jnp.where(lane < HEAD_DIM, values, zero)
    second = jnp.where(lane < HEAD_DIM, zero, values)
    return jnp.concatenate([first, second], axis=0)


def one_of_two(both):
    rows = both.shape[1] // 2
    at = lax.broadcasted_iota(jnp.int32, (both.shape[0], rows), 0)
    return jnp.where(at < HEAD_DIM, both[:, :rows], both[:, rows:]).T


def window_of(tok, lo, step):
    return tok + lo - MAX_DOC, MAX_DOC + step


def seen(start, tok, lo, step):
    first, size = window_of(tok, lo, step)
    key = lax.broadcasted_iota(jnp.int32, (size, step), 0) + first
    own = lax.broadcasted_iota(jnp.int32, (size, step), 1) + (tok + lo)
    allowed = (key >= start[:, lo : lo + step]) & (key <= own)
    bias = jnp.where(allowed, 0.0, MASKED)
    return jnp.concatenate([bias, bias], axis=1)


def attend_kernel(step, width, order, query, halo, own, start, w_out, *outs):
    attended, log_sum, send, keep, every = outs
    tok = query.shape[0]
    at = pl.program_id(0)
    keys = jnp.concatenate([halo[0], own[0]], axis=0)
    values = jnp.concatenate([halo[1], own[1]], axis=0).T
    for lo in range(0, tok, step):
        first, size = window_of(tok, lo, step)
        asked = two_heads(query[lo : lo + step, :])
        scores = mm(keys[first : first + size], asked, 1, 1) + seen(start, tok, lo, step)
        peak = jnp.max(scores, axis=0, keepdims=True)
        exponent = jnp.exp(scores - peak)
        mass = jnp.sum(exponent, axis=0, keepdims=True)
        prob = (exponent * (1.0 / mass)).astype(LOW)
        found = mm(values[:, first : first + size], prob, 1, 0)
        rows = one_of_two(found).astype(LOW)
        attended[lo : lo + step, :] = rows
        every[lo : lo + step, pl.ds(pl.multiple_of(at * PAIR, PAIR), PAIR)] = rows
        sums = peak + jnp.log(mass)
        log_sum[0, 0:1, lo : lo + step] = sums[:, :step]
        log_sum[0, 1:2, lo : lo + step] = sums[:, step:]

    @pl.when(at == pl.num_programs(0) - 1)
    def _():
        rows = every[...]
        for to in range(2):
            here = slice(to * width, (to + 1) * width)
            away = pl.ds(pl.multiple_of(order[to] * width, width), width)
            send[:, here] = mm(rows, w_out[:, away], 1, 0).astype(LOW)
            home = pl.ds(pl.multiple_of(order[2 + to] * width, width), width)
            keep[:, here] = mm(rows, w_out[:, home], 1, 0)


def attend(query, halo, own, start, w_out, order, width):
    tok, local = query.shape
    pairs = local // PAIR
    step = 128
    both = pl.BlockSpec((2, tok, PAIR), lambda p, s: (0, 0, p))
    wide = pl.BlockSpec((tok, 2 * width), lambda p, s: (0, 0))
    return pl.pallas_call(
        functools.partial(attend_kernel, step, width),
        grid_spec=pltpu.PrefetchScalarGridSpec(
            num_scalar_prefetch=1,
            grid=(pairs,),
            in_specs=[
                pl.BlockSpec((tok, PAIR), lambda p, s: (0, p)),
                both,
                both,
                whole_spec((1, tok)),
                whole_spec(w_out.shape),
            ],
            out_specs=[
                pl.BlockSpec((tok, PAIR), lambda p, s: (0, p)),
                pl.BlockSpec((1, 2, tok), lambda p, s: (p, 0, 0)),
                wide,
                wide,
            ],
            scratch_shapes=[pltpu.VMEM((tok, local), LOW)],
        ),
        out_shape=[
            shape_of((tok, local), LOW),
            shape_of((pairs, 2, tok), F32),
            shape_of((tok, 2 * width), LOW),
            shape_of((tok, 2 * width), F32),
        ],
        cost_estimate=cost(
            8 * tok * (MAX_DOC + step) * local + 8 * tok * local * width,
            12 * tok * local + 20 * tok * width,
            tok * local * 10,
        ),
        name="attend",
    )(order, query, halo, own, start, w_out)


def attend_back_kernel(count, step, owned, index, *refs):
    parts = refs[:count]
    w_out, query, halo, own, start, log_sum, cosine, sine = refs[count : count + 8]
    d_query, d_halo, d_own, row_keep, row_send, d_rows, d_keys, d_values = refs[count + 8 :]
    tok = query.shape[0]

    @pl.when(pl.program_id(0) == 0)
    def _():
        for at, part in enumerate(parts):
            width = part.shape[1]
            d_rows[:, pl.ds(pl.multiple_of((index[0] ^ at) * width, width), width)] = part[...]
        split_pairs(d_rows, owned, index[1] == 1, row_keep, row_send)

    d_attended = mm(d_rows[...], w_out[...], 1, 1).astype(LOW)
    keys = jnp.concatenate([halo[0], own[0]], axis=0)
    values = jnp.concatenate([halo[1], own[1]], axis=0)
    keys_across = keys.T
    d_keys[...] = jnp.zeros_like(d_keys)
    d_values[...] = jnp.zeros_like(d_values)
    for lo in range(0, tok, step):
        first, size = window_of(tok, lo, step)
        here = pl.ds(first, size)
        asked = two_heads(query[lo : lo + step, :])
        grads = two_heads(d_attended[lo : lo + step, :])
        sums = jnp.concatenate(
            [log_sum[0, 0:1, lo : lo + step], log_sum[0, 1:2, lo : lo + step]], axis=1
        )
        scores = mm(keys[first : first + size], asked, 1, 1) + seen(start, tok, lo, step)
        prob = jnp.exp(scores - sums)
        d_prob = mm(values[first : first + size], grads, 1, 1)
        delta = jnp.sum(prob * d_prob, axis=0, keepdims=True)
        d_scores = (prob * (d_prob - delta)).astype(LOW)
        d_values[here, :] += mm(prob.astype(LOW), grads, 1, 0)
        d_keys[here, :] += mm(d_scores, asked, 1, 0)
        found = one_of_two(mm(keys_across[:, first : first + size], d_scores, 1, 0))
        d_query[lo : lo + step, :] = turn(
            found * SCORE_SCALE, cosine[lo : lo + step, :], sine[lo : lo + step, :], -1.0
        ).astype(LOW)
    d_halo[0] = d_keys[:tok].astype(LOW)
    d_halo[1] = d_values[:tok].astype(LOW)
    d_own[0] = d_keys[tok:]
    d_own[1] = d_values[tok:]


def attend_back(parts, w_out, query, halo, own, start, log_sum, cosine, sine, index, owned):
    tok, local = query.shape
    count = len(parts)
    wide = w_out.shape[1]
    pairs = local // PAIR
    step = 128
    both = pl.BlockSpec((2, tok, PAIR), lambda p, s: (0, 0, p))
    return pl.pallas_call(
        functools.partial(attend_back_kernel, count, step, owned),
        grid_spec=pltpu.PrefetchScalarGridSpec(
            num_scalar_prefetch=1,
            grid=(pairs,),
            in_specs=[whole_spec(parts[0].shape)] * count
            + [
                pl.BlockSpec((PAIR, wide), lambda p, s: (p, 0)),
                pl.BlockSpec((tok, PAIR), lambda p, s: (0, p)),
                both,
                both,
                whole_spec((1, tok)),
                pl.BlockSpec((1, 2, tok), lambda p, s: (p, 0, 0)),
                whole_spec((tok, PAIR)),
                whole_spec((tok, PAIR)),
            ],
            out_specs=[
                pl.BlockSpec((tok, PAIR), lambda p, s: (0, p)),
                both,
                both,
                pl.BlockSpec((tok, wide // 2), lambda p, s: (0, 0)),
                pl.BlockSpec((tok, wide // 2), lambda p, s: (0, 0)),
            ],
            scratch_shapes=[
                pltpu.VMEM((tok, wide), LOW),
                pltpu.VMEM((2 * tok, PAIR), F32),
                pltpu.VMEM((2 * tok, PAIR), F32),
            ],
        ),
        out_shape=[
            shape_of((tok, local), LOW),
            shape_of((2, tok, local), LOW),
            shape_of((2, tok, local), F32),
            shape_of((tok, wide // 2), LOW),
            shape_of((tok, wide // 2), LOW),
        ],
        cost_estimate=cost(
            2 * tok * wide * local + 20 * tok * (MAX_DOC + step) * local,
            2 * wide * local + 24 * tok * local,
            tok * local * 10,
        ),
        name="attend_back",
    )(index, *parts, w_out, query, halo, own, start, log_sum, cosine, sine)


def finish_kernel(d_own, back, cosine, sine, out):
    d_key = d_own[0] + back[0].astype(F32)
    out[0] = turn(d_key, cosine[...], sine[...], -1.0).astype(LOW)
    out[1] = (d_own[1] + back[1].astype(F32)).astype(LOW)


def finish_keys(d_own, back, cosine, sine):
    both, tok, local = d_own.shape
    spec = pl.BlockSpec((2, tok, PAIR), lambda p: (0, 0, p))
    return pl.pallas_call(
        finish_kernel,
        grid=(local // PAIR,),
        in_specs=[spec, spec, whole_spec((tok, PAIR)), whole_spec((tok, PAIR))],
        out_specs=spec,
        out_shape=shape_of((2, tok, local), LOW),
        cost_estimate=cost(10 * tok * local, 16 * tok * local),
        name="finish_keys",
    )(d_own, back, cosine, sine)


def partial_kernel(count, added, order, *refs):
    lefts, rights = refs[:count], refs[count : 2 * count]
    rest = refs[2 * count :]
    total = None
    for left, right in zip(lefts, rights):
        part = mm(left[...], right[...], 1, 1)
        total = part if total is None else total + part
    if not added:
        rest[0][...] = total.astype(LOW)
        return
    got, send, keep = rest
    total = total + got[...].astype(F32)
    half = pl.num_programs(0) // 2

    @pl.when(pl.program_id(0) < half)
    def _():
        send[...] = total.astype(LOW)

    @pl.when(pl.program_id(0) >= half)
    def _():
        keep[...] = total


def partial_product(lefts, rights, order, width, got=None):
    tok = lefts[0].shape[-2]
    tile = width // 2
    per = width // tile
    left_specs, right_specs, flops, moved = [], [], 0, 0
    left_args = []
    for left, right in zip(lefts, rights):
        if isinstance(left, tuple):
            array, at = left[0], left[1]
            depth = array.shape[2]
            left_specs.append(
                pl.BlockSpec(
                    (pl.Squeezed(), tok, depth),
                    lambda i, s, at=at: (at, 0, 0),
                    pipeline_mode=pl.Buffered(1),
                )
            )
            left_args.append(array)
        else:
            depth = left.shape[1]
            left_specs.append(whole_spec((tok, depth)))
            left_args.append(left)
        right_specs.append(pl.BlockSpec((tile, depth), lambda i, s: (s[i // per] * per + i % per, 0)))
        flops += 4 * tok * width * depth
        moved += 4 * width * depth + 2 * tok * depth
    block = pl.BlockSpec((tok, tile), lambda i, s: (0, i))
    if got is None:
        extra_in, extra = [], []
        out_specs, out_shape = block, shape_of((tok, 2 * width), LOW)
    else:
        extra_in, extra = [block], [got]
        out_specs = [
            pl.BlockSpec((tok, tile), lambda i, s: (0, jnp.minimum(i, per - 1))),
            pl.BlockSpec((tok, tile), lambda i, s: (0, jnp.maximum(i - per, 0))),
        ]
        out_shape = [shape_of((tok, width), LOW), shape_of((tok, width), F32)]
    return pl.pallas_call(
        functools.partial(partial_kernel, len(lefts), got is not None),
        grid_spec=pltpu.PrefetchScalarGridSpec(
            num_scalar_prefetch=1,
            grid=(2 * per,),
            in_specs=left_specs + right_specs + extra_in,
            out_specs=out_specs,
        ),
        out_shape=out_shape,
        cost_estimate=cost(flops, moved + 6 * tok * width),
        name="partial_product",
    )(order, *left_args, *rights, *extra)


def column_order():
    shard = lax.axis_index(TP)
    core, chip = shard % 2, shard // 2
    order = [2 * (1 - chip) + 1 - core, 2 * chip + 1 - core, 2 * (1 - chip) + core, shard]
    return jnp.stack(order).astype(jnp.int32)


def finish_reduce(send, keep):
    total = keep + swap(send, TP, 1).astype(F32)
    width = total.shape[1] // 2
    return total[:, width:], swap(total[:, :width].astype(LOW), TP, 2)


def assemble(parts, whole, shard):
    if len(parts[0].shape) == 2:
        for at, part in enumerate(parts):
            width = part.shape[1]
            whole[:, pl.ds(pl.multiple_of((shard ^ at) * width, width), width)] = part[...]
        return
    for at, part in enumerate(parts):
        _, chips, cores, rows, width = part.shape
        for place in range(chips * cores):
            whole[at * rows : (at + 1) * rows, place * width : (place + 1) * width] = part[
                0, place // cores, place % cores
            ]


def part_specs(parts, places):
    if places is None:
        rows, width = parts[0].shape
        return [whole_spec(part.shape) for part in parts], rows, len(parts) * width
    _, chips, cores, rows, width = parts[0].shape
    specs = [
        pl.BlockSpec(
            (1, chips, cores, rows, width),
            lambda h, s, place=place: (s[2 + place], 0, 0, 0, 0),
            pipeline_mode=pl.Buffered(1),
        )
        for place in places
    ]
    return specs, rows * len(places), chips * cores * width


def pick_owned(whole, owned, place, segments):
    size = owned.shape[1] // segments
    every = whole.shape[1] // segments
    for at in range(segments):
        first = pl.multiple_of(at * every + place * size, size)
        owned[:, at * size : (at + 1) * size] = whole[:, pl.ds(first, size)]


def back_units_kernel(count, segments, index, *refs):
    parts = refs[:count]
    w_down, d_inner, owned, whole = refs[count:]

    @pl.when(pl.program_id(0) == 0)
    def _():
        assemble(parts, whole, index[0])
        pick_owned(whole, owned, index[1], segments)

    d_inner[...] = mm(whole[...], w_down[...], 1, 1).astype(LOW)


def back_units(parts, places, w_down, index, ring, segments):
    specs, rows, wide = part_specs(parts, places)
    count = len(specs)
    parts = parts * (count // len(parts))
    units = w_down.shape[0]
    tile = min(512, units)
    return pl.pallas_call(
        functools.partial(back_units_kernel, count, segments),
        grid_spec=pltpu.PrefetchScalarGridSpec(
            num_scalar_prefetch=1,
            grid=(units // tile,),
            in_specs=specs + [pl.BlockSpec((tile, wide), lambda h, s: (h, 0))],
            out_specs=[
                pl.BlockSpec((rows, tile), lambda h, s: (0, h)),
                pl.BlockSpec((rows, wide // ring), lambda h, s: (0, 0)),
            ],
            scratch_shapes=[pltpu.VMEM((rows, wide), LOW)],
        ),
        out_shape=[shape_of((rows, units), LOW), shape_of((rows, wide // ring), LOW)],
        cost_estimate=cost(2 * rows * wide * units, 2 * wide * units + 2 * rows * (wide + units)),
        name="back_units",
    )(index, *parts, w_down)


def units_of(rows, w_gate, w_up, d_inner):
    gate = mm(rows, w_gate, 1, 0)
    up = mm(rows, w_up, 1, 0)
    sig = jax.nn.sigmoid(gate)
    held = gate * sig
    d_inner = d_inner.astype(F32)
    inner = (held * up).astype(LOW)
    d_gate = (d_inner * up * sig * (1.0 + gate * (1.0 - sig))).astype(LOW)
    return inner, d_gate, (d_inner * held).astype(LOW)


def far_units_kernel(count, segments, index, *refs):
    parts = refs[:count]
    d_inner, w_gate, w_up, inner, d_gate, d_up, owned, whole = refs[count:]

    @pl.when(pl.program_id(0) == 0)
    def _():
        assemble(parts, whole, index[0])
        pick_owned(whole, owned, index[1], segments)

    inner[...], d_gate[...], d_up[...] = units_of(
        whole[...], w_gate[...], w_up[...], d_inner[...]
    )


def far_units(parts, places, d_inner, w_gate, w_up, index, ring, segments):
    specs, rows, wide = part_specs(parts, places)
    count = len(specs)
    parts = parts * (count // len(parts))
    units = w_gate.shape[1]
    tile = min(512, units)
    unit = pl.BlockSpec((rows, tile), lambda h, s: (0, h))
    weight = pl.BlockSpec((wide, tile), lambda h, s: (0, h))
    return pl.pallas_call(
        functools.partial(far_units_kernel, count, segments),
        grid_spec=pltpu.PrefetchScalarGridSpec(
            num_scalar_prefetch=1,
            grid=(units // tile,),
            in_specs=specs + [unit, weight, weight],
            out_specs=[unit] * 3 + [pl.BlockSpec((rows, wide // ring), lambda h, s: (0, 0))],
            scratch_shapes=[pltpu.VMEM((rows, wide), LOW)],
        ),
        out_shape=[shape_of((rows, units), LOW)] * 3 + [shape_of((rows, wide // ring), LOW)],
        cost_estimate=cost(
            4 * rows * wide * units, 4 * wide * units + 8 * rows * units, rows * units
        ),
        name="far_units",
    )(index, *parts, d_inner, w_gate, w_up)


def own_units_kernel(count, segments, index, order, *refs):
    parts, grad_parts = refs[:count], refs[count : count + 1]
    w_gate, w_up, w_down, inner, d_gate, d_up, owned, grad_owned = refs[count + 1 : count + 9]
    back_send, back_keep, out_send, out_keep, whole, grads, back_sum, out_sum = refs[count + 9 :]
    step = pl.program_id(0)
    wide = whole.shape[1]
    width = parts[0].shape[1]

    @pl.when(step == 0)
    def _():
        assemble(parts, whole, index[0])
        pick_owned(whole, owned, index[1], segments)
        assemble(grad_parts, grads, index[0])
        pick_owned(grads, grad_owned, index[1], segments)
        back_sum[...] = jnp.zeros_like(back_sum)
        out_sum[...] = jnp.zeros_like(out_sum)

    d_inner = mm(grads[...], w_down[...], 1, 1)
    units = units_of(whole[...], w_gate[...], w_up[...], d_inner)
    inner[...], d_gate[...], d_up[...] = units
    for lo in range(0, wide, width):
        here = slice(lo, lo + width)
        back_sum[:, here] += mm(units[1], w_gate[here, :], 1, 1) + mm(units[2], w_up[here, :], 1, 1)
        out_sum[:, here] += mm(units[0], w_down[:, here], 1, 0)

    @pl.when(step == pl.num_programs(0) - 1)
    def _():
        for to in range(2):
            here = slice(to * width, (to + 1) * width)
            away = pl.ds(pl.multiple_of(order[to] * width, width), width)
            home = pl.ds(pl.multiple_of(order[2 + to] * width, width), width)
            back_send[:, here] = back_sum[:, away].astype(LOW)
            back_keep[:, here] = back_sum[:, home]
            out_send[:, here] = out_sum[:, away].astype(LOW)
            out_keep[:, here] = out_sum[:, home]


def own_units(parts, grad_every, w_gate, w_up, w_down, index, order, ring, segments):
    count = len(parts)
    rows, width = parts[0].shape
    wide, units = w_gate.shape
    tile = min(256, units)
    unit = pl.BlockSpec((rows, tile), lambda h, s, o: (0, h))
    weight = pl.BlockSpec((wide, tile), lambda h, s, o: (0, h))
    half = pl.BlockSpec((rows, 2 * width), lambda h, s, o: (0, 0))
    mine = pl.BlockSpec((rows, wide // ring), lambda h, s, o: (0, 0))
    grads = pl.BlockSpec(
        (1,) + grad_every.shape[1:],
        lambda h, s, o: (s[1], 0, 0, 0, 0),
        pipeline_mode=pl.Buffered(1),
    )
    return pl.pallas_call(
        functools.partial(own_units_kernel, count, segments),
        grid_spec=pltpu.PrefetchScalarGridSpec(
            num_scalar_prefetch=2,
            grid=(units // tile,),
            in_specs=[whole_spec((rows, width))] * count
            + [grads, weight, weight, pl.BlockSpec((tile, wide), lambda h, s, o: (h, 0))],
            out_specs=[unit] * 3 + [mine] * 2 + [half] * 4,
            scratch_shapes=[
                pltpu.VMEM((rows, wide), LOW),
                pltpu.VMEM((rows, wide), LOW),
                pltpu.VMEM((rows, wide), F32),
                pltpu.VMEM((rows, wide), F32),
            ],
        ),
        out_shape=[shape_of((rows, units), LOW)] * 3
        + [shape_of((rows, wide // ring), LOW)] * 2
        + [shape_of((rows, 2 * width), LOW), shape_of((rows, 2 * width), F32)] * 2,
        cost_estimate=cost(
            12 * rows * wide * units, 6 * wide * units + 8 * rows * units, rows * units
        ),
        name="own_units",
    )(index, order, *parts, grad_every, w_gate, w_up, w_down)


def ffn_grads_kernel(owned, counts, seat, *refs):
    groups, at = [], 0
    for count in counts:
        groups.append(refs[at : at + count])
        at += count
    normed, grads, d_gate, d_up, inner = groups
    send, keep, normed_across, grads_across = refs[at:]

    @pl.when(pl.program_id(0) == 0)
    def _():
        other = seat[0] == 1
        for parts, across in ((normed, normed_across), (grads, grads_across)):
            lo = 0
            for part in parts:
                rows = part.shape[0]
                whole = part[...]
                first, second = whole[:, :owned].T, whole[:, owned:].T
                across[:owned, lo : lo + rows] = jnp.where(other, first, second)
                across[owned:, lo : lo + rows] = jnp.where(other, second, first)
                lo += rows

    for to, (across, parts) in enumerate(
        ((normed_across, d_gate), (normed_across, d_up), (grads_across, inner))
    ):
        total, lo = None, 0
        for part in parts:
            rows = part.shape[0]
            term = mm(across[:, lo : lo + rows], part[...], 1, 0)
            total = term if total is None else total + term
            lo += rows
        send[to] = total[:owned].astype(LOW)
        keep[to] = total[owned:]


def ffn_grads(normed, grads, d_gate, d_up, inner, seat, owned):
    groups = [normed, grads, d_gate, d_up, inner]
    counts = [len(group) for group in groups]
    rows = sum(part.shape[0] for part in normed)
    units = inner[0].shape[1]
    tile = min(512, units)
    specs = []
    for group in groups[:2]:
        specs += [whole_spec((part.shape[0], 2 * owned)) for part in group]
    for group in groups[2:]:
        specs += [pl.BlockSpec((part.shape[0], tile), lambda h, s: (0, h)) for part in group]
    stack = pl.BlockSpec((3, owned, tile), lambda h, s: (0, 0, h))
    return pl.pallas_call(
        functools.partial(ffn_grads_kernel, owned, counts),
        grid_spec=pltpu.PrefetchScalarGridSpec(
            num_scalar_prefetch=1,
            grid=(units // tile,),
            in_specs=specs,
            out_specs=[stack, stack],
            scratch_shapes=[pltpu.VMEM((2 * owned, rows), LOW)] * 2,
        ),
        out_shape=[shape_of((3, owned, units), LOW), shape_of((3, owned, units), F32)],
        cost_estimate=cost(12 * rows * owned * units, 6 * rows * units + 18 * owned * units),
        name="ffn_grads",
    )(seat[None].astype(jnp.int32), *[part for group in groups for part in group])


def add_grads_kernel(keep, got, gate, up, down):
    gate[...] = keep[0] + got[0].astype(F32)
    up[...] = keep[1] + got[1].astype(F32)
    down[...] = (keep[2] + got[2].astype(F32)).T


def add_grads(keep, got):
    _, owned, units = keep.shape
    tile = min(512, units)
    stack = pl.BlockSpec((3, owned, tile), lambda h: (0, 0, h))
    wide = pl.BlockSpec((owned, tile), lambda h: (0, h))
    return pl.pallas_call(
        add_grads_kernel,
        grid=(units // tile,),
        in_specs=[stack, stack],
        out_specs=[wide, wide, pl.BlockSpec((tile, owned), lambda h: (h, 0))],
        out_shape=[shape_of((owned, units), F32)] * 2 + [shape_of((units, owned), F32)],
        cost_estimate=cost(3 * owned * units, 30 * owned * units),
        name="add_grads",
    )(keep, got)


def per_device(
    block_input,
    grad_output,
    norm_attn,
    norm_ffn,
    w_query,
    w_key,
    w_value,
    w_out,
    w_gate,
    w_up,
    w_down,
    doc_lengths,
):
    tok, width = block_input.shape
    width_all = norm_attn.shape[0]
    n_dp = lax.axis_size(DP)
    me = lax.axis_index(DP)
    shard = lax.axis_index(TP)
    ring = min(RING, n_dp // 2)
    blocks = n_dp // (2 * ring)
    pair_at = me % 2
    ring_at = (me // 2) % ring
    block_at = me // (2 * ring)
    owned = width_all // n_dp
    seat = block_at * 2 + pair_at
    seats = blocks * 2
    index = jnp.stack([shard, pair_at]).astype(jnp.int32)
    ring_index = jnp.stack(
        [shard, ring_at] + [(ring_at + step) % ring for step in range(1, ring)]
    ).astype(jnp.int32)

    def seat_swap(values, mask):
        pairs = []
        for i in range(n_dp):
            b, k, c = i // (2 * ring), (i // 2) % ring, i % 2
            s = (b * 2 + c) ^ mask
            pairs.append((i, ((s // 2) * ring + k) * 2 + s % 2))
        return lax.ppermute(values, DP, pairs)

    row_groups = ROW_LEN // tok
    halo_pairs = [(i, i + 1) for i in range(n_dp) if 0 < i % row_groups < row_groups - 1]
    back_pairs = [(j, i) for i, j in halo_pairs]

    starts = jnp.cumsum(doc_lengths, dtype=jnp.int32) - doc_lengths
    token_ids = (me - 1) * tok + jnp.arange(2 * tok, dtype=jnp.int32)
    doc_start = jnp.max(
        jnp.where(starts[:, None] <= token_ids[None, :], starts[:, None], 0), axis=0
    )
    position = (token_ids - doc_start).astype(F32)
    start = (doc_start[tok:] - (me - 1) * tok)[None, :]
    lane = jnp.arange(PAIR, dtype=jnp.int32) % (HEAD_DIM // 2)
    frequency = THETA ** (-lane.astype(F32) * 2.0 / HEAD_DIM)
    angles = position[:, None] * frequency[None, :]
    cosine, sine = jnp.cos(angles[tok:]), jnp.sin(angles[tok:])
    halo_cosine, halo_sine = jnp.cos(angles[:tok]), jnp.sin(angles[:tok])

    my_gain_one = lax.dynamic_slice_in_dim(norm_attn, shard * width, width)
    my_gain_two = lax.dynamic_slice_in_dim(norm_ffn, shard * width, width)
    my_rows = block_input.astype(F32)
    my_grad = grad_output.astype(F32)

    order = column_order()
    away, home = order[:2], order[2:]

    def ring_send(values, shift):
        pairs = []
        for i in range(n_dp):
            b, k, c = i // (2 * ring), (i // 2) % ring, i % 2
            pairs.append((i, (b * ring + (k + shift) % ring) * 2 + c))
        return lax.ppermute(values, DP, pairs)

    def after(values, *others):
        return lax.optimization_barrier((values, *others))[0]

    row_parts = gather_blocks(block_input)
    halo_rows = lax.ppermute(block_input, DP, halo_pairs)
    halo_parts = gather_blocks(halo_rows)
    grad_every = lax.all_gather(after(grad_output, halo_rows, row_parts[-2]), ("ring",) + TP, axis=0)
    grad_every = grad_every.reshape(ring, lax.axis_size("chip"), 2, tok, width)

    query, own, normed_keep, normed_send, scale_wide = project_in(
        row_parts, norm_attn, cosine, sine, w_query, w_key, w_value, index, owned
    )
    scale_one = scale_wide[:, :1]
    normed_far = swap(normed_send, "pair", 1)
    halo = project_halo(
        halo_parts, norm_attn, halo_cosine, halo_sine, w_key, w_value, index
    )
    attended, log_sum, send, keep = attend(query, halo, own, start, w_out, order, width)
    send = after(send, normed_far)

    mine, come = finish_reduce(send, keep)
    hidden = my_rows + (mine + come.astype(F32))
    square = sum_all(jnp.sum(hidden * hidden, axis=1), TP)
    scale_two = lax.rsqrt(square / width_all + EPS)[:, None]
    normed_slice = (hidden * scale_two * my_gain_two).astype(LOW)
    normed_parts = gather_blocks(normed_slice)
    normed_every = lax.all_gather(normed_slice, ("ring",) + TP, axis=0)
    normed_every = normed_every.reshape(ring, lax.axis_size("chip"), 2, tok, width)

    found = own_units(
        normed_parts, grad_every, w_gate, w_up, w_down, ring_index, order, ring, blocks
    )
    pieces, units_grad = [found[:4]], [found[4]]
    send, keep, out_send, out_keep = found[5:]
    groups = [range(ring - 1)] if ring < 3 else [range(1), range(1, ring - 1)]

    def more_units(at, *waits):
        grads, rows = after(grad_every, *waits), after(normed_every, *waits)
        d_inner, grad_owned = back_units([grads], groups[at], w_down, ring_index, ring, blocks)
        found = far_units(
            [rows], groups[at], d_inner, w_gate, w_up, ring_index, ring, blocks
        )
        pieces.append(found)
        units_grad.append(grad_owned)
        return d_inner, found[0]

    first_back, first_units = more_units(0, send)

    mine, come = finish_reduce(send, keep)
    come = after(come, first_back)
    d_normed_two = mine + come.astype(F32)
    gain_two = jnp.sum(d_normed_two * hidden * scale_two, axis=0)
    weighted = d_normed_two * my_gain_two
    mean_two = sum_all(jnp.sum(weighted * hidden, axis=1), TP) / width_all
    d_hidden = my_grad + scale_two * (
        weighted - hidden * scale_two * scale_two * mean_two[:, None]
    )
    d_hidden_parts = after(gather_blocks(d_hidden.astype(LOW)), first_units)

    d_query, d_halo, d_own, hidden_keep, hidden_send = attend_back(
        d_hidden_parts, w_out, query, halo, own, start, log_sum, cosine, sine, index, owned
    )
    back = lax.ppermute(d_halo, DP, back_pairs)
    out_come = swap(mm(attended, hidden_send, 0, 0).astype(LOW), "pair", 1)
    far_query = swap(d_query, "pair", 1)
    if len(groups) > 1:
        back = after(back, more_units(1, d_query)[1])
    d_both = finish_keys(d_own, back, cosine, sine)
    far_both = swap(d_both, "pair", 1)
    units, units_gate, units_up, units_normed = (list(part) for part in zip(*pieces))

    if owned % 128 == 0 and seats == 2:
        units_gate[-1] = after(units_gate[-1], d_both)
        far_send, near_keep = ffn_grads(
            units_normed, units_grad, units_gate, units_up, units, seat, owned
        )
        d_both, out_come, far_query = after((d_both, out_come, far_query), far_send)
        grad_gate, grad_up, grad_down = add_grads(near_keep, seat_swap(far_send, 1))
    else:

        def seat_grads(at):
            def columns(rows):
                return lax.dynamic_slice_in_dim(rows, at * owned, owned, 1)

            def product(rows, hidden_units):
                return mm(columns(jnp.concatenate(rows)), jnp.concatenate(hidden_units), 0, 0)

            return jnp.stack(
                [
                    product(units_normed, units_gate),
                    product(units_normed, units_up),
                    product(units_grad, units),
                ]
            )

        total = seat_grads(seat)
        for mask in range(1, seats):
            total = total + seat_swap(seat_grads(seat ^ mask).astype(LOW), mask).astype(F32)
        grad_gate, grad_up, grad_down = total[0], total[1], total[2].T

    lefts = [d_query, (d_both, 0), (d_both, 1)]
    rights = [w_query, w_key, w_value]
    sent = partial_product(lefts, rights, away, width)
    send, mine = partial_product(lefts, rights, home, width, swap(sent, TP, 1))
    d_normed_one = mine + swap(send, TP, 2).astype(F32)
    gain_one = jnp.sum(d_normed_one * my_rows * scale_one, axis=0)
    weighted = d_normed_one * my_gain_one
    mean_one = sum_all(jnp.sum(weighted * my_rows, axis=1), TP) / width_all
    d_rows = d_hidden + scale_one * (
        weighted - my_rows * scale_one * scale_one * mean_one[:, None]
    )
    grad_input = d_rows.astype(LOW)

    mine, come = finish_reduce(out_send, out_keep)
    block_output = (hidden + (mine + come.astype(F32))).astype(LOW)

    def around(total, axis):
        mine = lax.dynamic_index_in_dim(total, ring_at, axis, False)
        for shift in range(1, ring):
            other = lax.dynamic_index_in_dim(total, (ring_at + shift) % ring, axis, False)
            mine = mine + ring_send(other.astype(LOW), shift).astype(F32)
        total = mine
        mine = lax.dynamic_index_in_dim(total, block_at, axis - 1, False)
        for mask in range(1, blocks):
            other = lax.dynamic_index_in_dim(total, block_at ^ mask, axis - 1, False)
            mine = mine + swap(other.astype(LOW), DP, mask * 2 * ring).astype(F32)
        return mine

    total = mm(attended, hidden_keep, 0, 0) + out_come.astype(F32)
    grad_wout = around(total.reshape(-1, blocks, ring, owned), 2)

    def in_grad(near, far):
        total = mm(normed_keep, near, 0, 0) + mm(normed_far, far, 0, 0)
        return total.reshape(blocks, ring, owned, -1)

    grad_query = around(in_grad(d_query, far_query), 1)
    pair_grads = around(
        jnp.concatenate(
            [in_grad(d_both[0], far_both[0]), in_grad(d_both[1], far_both[1])], axis=3
        ),
        1,
    )
    local = d_query.shape[1]
    grad_key, grad_value = pair_grads[:, :local], pair_grads[:, local:]

    gains = sum_all(jnp.stack([gain_one, gain_two]), DP)
    gain_parts = gather_blocks(gains)
    gains = jnp.zeros((2, width_all), F32)
    for at, part in enumerate(gain_parts):
        gains = lax.dynamic_update_slice(gains, part, (0, (shard ^ at) * width))
    return (
        block_output,
        grad_input,
        gains[0],
        gains[1],
        grad_query,
        grad_key,
        grad_value,
        grad_wout,
        grad_gate,
        grad_up,
        grad_down,
    )


def solution(mesh):
    n_dp, n_tp = mesh.shape["dp"], mesh.shape["tensor"]
    ring = min(RING, n_dp // 2)
    parts = mesh.devices.reshape(n_dp // (2 * ring), ring, 2, n_tp // 2, 2)
    finer = Mesh(parts, DP + TP)
    rows, cols = P(DP, TP), P(TP, DP)
    wide, tall = P(None, TP), P(TP, None)
    return jax.shard_map(
        per_device,
        mesh=finer,
        in_specs=(rows, rows, P(), P(), wide, wide, wide, tall, wide, wide, tall, P()),
        out_specs=(rows, rows, P(), P(), rows, rows, rows, cols, rows, rows, cols),
        check_vma=False,
    )
```
